32 devices in a mesh: seg: 4 (over z), sec: 8 (over y, x, core).
Axes of the slice: x: 2, y: 2, z: 4, core: 2. Of those that a mesh axis runs over, the one named last changes fastest.
Arguments:
- start_vector: float32 [4, 1024, 2, 1024], P('seg', 'sec'), may hold values from -6 to 6
- left_env: bfloat16 [4, 5, 1024, 1024], P('seg', None, 'sec'), as said below
- right_env: bfloat16 [4, 5, 1024, 1024], P('seg', None, 'sec'), as said below
- charge_left: int32 [4, 1024], P('seg', 'sec'), may hold values from -8 to 8, as said below
- charge_right: int32 [4, 1024], P('seg'), may hold values from -8 to 8, as said below
Outputs:
- final_vector: float32 [4, 1024, 2, 1024], P('seg', 'sec')
- coefficients: float32 [4, 4], P('seg')
The draws below stay inside these ranges and needn't reach their ends.
Inputs may be any that keep to these rules, and one draw needn't show every extreme that they name: `charge_left`: each segment's left bond holds both charges -8 and 8; charges gather near 0. `charge_right`: each segment's right bond holds both charges -8 and 8; charges gather near 0. left_env[g] is zero outside the charge rule stated for it, with the charges charge_left[(g + 1) mod 4]. right_env[g] is zero outside the charge rule stated for it, with the charges charge_right[(g - 1) mod 4].
All inputs are finite; a program needn't handle non-finite values.
Results may differ from the reference program's by a relative error of at most 0.0042.
Values may be sent and summed in bfloat16 or wider, within the bound.
A program may use at most 128 MiB of HBM per device.

```python
import jax
import jax.numpy as jnp
import numpy as np
from jax import lax

CHI = 1024
ITERS = 4
SEGS = 4
N_SEG = 4


def bond_charges(key, salt):
    inner = jax.random.fold_in(key, salt)
    first_key, second_key, order_key = jax.random.split(inner, 3)
    first = jax.random.randint(first_key, (SEGS, CHI - 2), -4, 5, dtype=jnp.int32)
    second = jax.random.randint(second_key, (SEGS, CHI - 2), -4, 5, dtype=jnp.int32)
    values = jnp.concatenate([jnp.full((SEGS, 1), -8, jnp.int32), jnp.full((SEGS, 1), 8, jnp.int32), first + second], axis=1)
    row_key_labels = jax.random.split(order_key, SEGS)
    return jax.vmap(lambda row_key, row: jax.random.permutation(row_key, row))(row_key_labels, values)


def env_values(key, used_charges):
    lanczos_step_table = jnp.asarray(np.array([0, -1, 1, 0, 0], np.int32))
    differ = used_charges[:, :, None] - used_charges[:, None, :]
    keep = (differ[:, None, :, :] == lanczos_step_table[None, :, None, None]).astype(jnp.float32)
    value_key = jax.random.fold_in(key, 31)
    values = jnp.clip(jax.random.normal(value_key, (SEGS, 5, CHI, CHI), jnp.float32), -6.0, 6.0)
    return (values * keep * (3.5 / np.sqrt(CHI))).astype(jnp.bfloat16)


def draw_charge_left(key, part):
    return bond_charges(key, 11)


def draw_charge_right(key, part):
    return bond_charges(key, 12)


def draw_left_env(key, part):
    used = jnp.roll(bond_charges(key, 11), -1, axis=0)
    return env_values(jax.random.fold_in(key, 21), used)


def draw_right_env(key, part):
    used = jnp.roll(bond_charges(key, 12), 1, axis=0)
    return env_values(jax.random.fold_in(key, 22), used)


def shard_levels(key, shape, cuts, smallest, largest):
    def one(position, parts):
        heights = jax.random.uniform(jax.random.fold_in(jax.random.fold_in(key, 6), position), (parts,), jnp.float32, smallest / len(cuts), largest / len(cuts))
        return jnp.repeat(jnp.exp(heights), shape[position] // parts).reshape((-1,) + (1,) * (len(shape) - position - 1))

    loudness = one(*cuts[0])
    for cut in cuts[1:]:
        loudness = loudness * one(*cut)
    return loudness


def scatter_about(stream_key, extent, deviation, limit, cuts=(), kind=jnp.bfloat16):
    factor_of = shard_levels(stream_key, extent, cuts, -0.22, 0.18) if cuts else 1.0
    values = jax.random.normal(stream_key, extent, jnp.float32) * deviation * factor_of
    return jnp.minimum(jnp.maximum(values, -limit), limit).astype(kind)


def setup_inputs(seed: int = 0) -> dict:
    splits = jax.random.split(jax.random.key(seed), 6)
    start_vector = scatter_about(splits[0], (SEGS, CHI, 2, CHI), 1.0, 6.0, ((0, 4), (1, 8)), jnp.float32)
    left_env = draw_left_env(jax.random.fold_in(splits[5], 71), 0)
    right_env = draw_right_env(jax.random.fold_in(splits[5], 71), 0)
    charge_left = draw_charge_left(jax.random.fold_in(splits[5], 71), 0)
    charge_right = draw_charge_right(jax.random.fold_in(splits[5], 71), 0)
    return {"start_vector": start_vector, "left_env": left_env, "right_env": right_env, "charge_left": charge_left, "charge_right": charge_right}


EPS = 1e-06

def mpo_table():
    identity = np.eye(2, dtype=np.float32)
    raising = np.array([[0.0, 0.0], [1.0, 0.0]], np.float32)
    lowering = np.array([[0.0, 1.0], [0.0, 0.0]], np.float32)
    diagonal_spin = np.array([[-0.5, 0.0], [0.0, 0.5]], np.float32)
    table = np.zeros((5, 5, 2, 2), np.float32)
    table[0, 0] = identity
    table[1, 0] = raising
    table[2, 0] = lowering
    table[3, 0] = diagonal_spin
    table[4, 1] = 0.5 * lowering
    table[4, 2] = 0.5 * raising
    table[4, 3] = diagonal_spin
    table[4, 4] = identity
    return table

def reference(start_vector, left_env, right_env, charge_left, charge_right):
    operator_table = jnp.asarray(mpo_table(), jnp.float32)
    spin_values = jnp.arange(2, dtype=jnp.int32)
    finals = []
    betas_all = []
    for group in range(N_SEG):
        left_block_tensor = left_env[(group - 1) % N_SEG].astype(jnp.float32)
        right_whole = right_env[(group + 1) % N_SEG].astype(jnp.float32)
        permitted_entries = (charge_right[group][None, None, :] == charge_left[group][:, None, None] + spin_values[None, :, None]).astype(jnp.float32)
        current = start_vector[group] * permitted_entries
        current = current / jnp.sqrt(jnp.sum(current * current) + EPS)
        previous = jnp.zeros_like(current)
        length_now = jnp.float32(0.0)
        lengths = []
        for iteration in range(ITERS):
            rounded_result = lax.optimization_barrier(current.astype(jnp.bfloat16))
            rounded_result = rounded_result.astype(jnp.float32)
            partial_left_contraction = jnp.einsum('bkj,jet->bket', left_block_tensor, rounded_result, precision=lax.Precision.HIGHEST)
            mixed_terms = jnp.einsum('abyx,alxr->blyr', operator_table, partial_left_contraction, precision=lax.Precision.HIGHEST)
            mixed_terms = lax.optimization_barrier(mixed_terms.astype(jnp.bfloat16)).astype(jnp.float32)
            operator_image = jnp.einsum('blyr,brq->lyq', mixed_terms, right_whole, precision=lax.Precision.HIGHEST) * permitted_entries
            residual = operator_image - length_now * previous
            correlation = jnp.sum(residual * current)
            residual = residual - correlation * current
            length_now = jnp.sqrt(jnp.sum(residual * residual) + EPS)
            previous = current
            current = residual / length_now
            lengths.append(length_now)
        finals.append(current * CHI)
        betas_all.append(jnp.stack(lengths))
    return (jnp.stack(finals), jnp.stack(betas_all))
```

```python
import jax
import jax.numpy as jnp
from jax import lax
from jax.sharding import PartitionSpec as P

CHI = 1024
ITERS = 4


EPS = 1e-06


def shifted(value, axis, steps):
    count = lax.axis_size(axis)
    pairs = [(source, (source + steps) % count) for source in range(count)]
    return lax.ppermute(value, axis, pairs)


def merged(env):
    return jnp.stack([env[0] + env[1] + env[2], env[3], env[4]])


def on_device(start_vector, left_env, right_env, charge_left, charge_right):
    left = shifted(merged(left_env[0]), "seg", 1)
    passed = shifted(merged(right_env[0]), "seg", -1)
    right = lax.all_gather(passed, "sec", axis=1, tiled=True)
    charges = charge_right[0]
    step = charges[None, :] - charges[:, None]
    right_stack = jnp.concatenate(
        [
            jnp.where(step == 0, right[0], 0),
            jnp.where(step == 1, right[0], 0),
            jnp.where(step == -1, right[0], 0),
            right[1],
            right[2],
        ],
        axis=0,
    )
    gap = charges[None, :] - charge_left[0][:, None]
    down, up = gap == 0, gap == 1
    allowed = down | up
    spin = jnp.where(up, 0.5, -0.5)
    rows = gap.shape[0]
    left_rows = left.reshape(3 * rows, left.shape[2])

    current = jnp.where(down, start_vector[0, :, 0], jnp.where(up, start_vector[0, :, 1], 0.0))
    norm = lax.psum(jnp.sum(current * current), "sec")
    current = current / jnp.sqrt(norm + EPS)
    previous = jnp.zeros_like(current)
    beta = jnp.float32(0.0)
    betas = []
    for _ in range(ITERS):
        whole = lax.all_gather(current.astype(jnp.bfloat16), "sec", axis=0, tiled=True)
        first = jnp.dot(left_rows, whole, preferred_element_type=jnp.float32)
        first = first.reshape(3, rows, -1)
        half = 0.5 * first[2]
        mixed = jnp.concatenate(
            [
                jnp.where(allowed, first[0] + spin * first[1], 0.0),
                jnp.where(up, half, 0.0),
                jnp.where(down, half, 0.0),
                jnp.where(allowed, spin * first[2], 0.0),
                jnp.where(allowed, first[2], 0.0),
            ],
            axis=1,
        ).astype(jnp.bfloat16)
        image = jnp.dot(mixed, right_stack, preferred_element_type=jnp.float32)
        residual = jnp.where(allowed, image, 0.0) - beta * previous
        alpha = lax.psum(jnp.sum(residual * current), "sec")
        residual = residual - alpha * current
        beta = jnp.sqrt(lax.psum(jnp.sum(residual * residual), "sec") + EPS)
        previous = current
        current = residual / beta
        betas.append(beta)
    scaled = current * CHI
    final = jnp.stack([jnp.where(down, scaled, 0.0), jnp.where(up, scaled, 0.0)], axis=1)
    return final[None], jnp.stack(betas)[None]


def solution(mesh):
    return jax.shard_map(
        on_device,
        mesh=mesh,
        in_specs=(
            P("seg", "sec", None, None),
            P("seg", None, "sec", None),
            P("seg", None, "sec", None),
            P("seg", "sec"),
            P("seg", None),
        ),
        out_specs=(P("seg", "sec", None, None), P("seg", None)),
        check_vma=False,
    )
```

```python
import functools

import jax
import jax.numpy as jnp
from jax import lax
from jax.experimental import pallas as pl
from jax.experimental.pallas import tpu as pltpu
from jax.sharding import PartitionSpec as P

CHI = 1024
ITERS = 4
EPS = 1e-06
MESH = pl.DeviceIdType.MESH
TILE = 256


def merged(env):
    return jnp.stack([env[0] + env[1] + env[2], env[3], env[4]])


def kernel(
    n,
    segs,
    left_ref,
    right_ref,
    start_ref,
    row_ref,
    col_ref,
    mine_ref,
    final_ref,
    beta_ref,
    left_buf,
    raw,
    split,
    whole,
    first,
    mixed,
    current,
    previous,
    vector,
    parts,
    left_send,
    left_recv,
    shift_send,
    shift_recv,
    right_send,
    right_recv,
    pass_send,
    pass_recv,
    vec_send,
    vec_recv,
    fwd_send,
    fwd_recv,
    part_send,
    part_recv,
):
    me = lax.axis_index("sec")
    seg = lax.axis_index("seg")
    rows, width = start_ref.shape
    chips = n // 2
    partner = me + 1 - 2 * lax.rem(me, 2)
    after, before = lax.rem(seg + 1, segs), lax.rem(seg + segs - 1, segs)

    def source(k):
        return lax.rem(me - 2 * k + n, n)

    def target(k):
        return lax.rem(me + 2 * k, n)

    def block(index):
        return pl.ds(pl.multiple_of(index * rows, rows), rows)

    barrier = pltpu.get_barrier_semaphore()
    for k in range(1, n):
        pl.semaphore_signal(barrier, inc=1, device_id={"sec": lax.rem(me + k, n)}, device_id_type=MESH)
    for other in (after, before):
        pl.semaphore_signal(barrier, inc=1, device_id={"seg": other}, device_id_type=MESH)
    pl.semaphore_wait(barrier, n + 1)

    def remote(src, dst, send, recv, where):
        return pltpu.make_async_remote_copy(
            src_ref=src, dst_ref=dst, send_sem=send, recv_sem=recv, device_id=where, device_id_type=MESH
        )

    left_copy = remote(left_ref, left_buf, left_send, left_recv, {"seg": after})
    shifts = [
        remote(right_ref.at[c], raw.at[c, block(me)], shift_send.at[c], shift_recv.at[c], {"seg": before})
        for c in range(3)
    ]

    def right_copy(c, k, owner):
        part = raw.at[c, block(owner)]
        return remote(part, part, right_send.at[c, k], right_recv.at[c, k], {"sec": target(k)})

    def right_pass(c, k):
        part = raw.at[c, block(source(k))]
        return remote(part, part, pass_send.at[c, k], pass_recv.at[c, k], {"sec": partner})

    def vec_copy(it, k):
        part = whole.at[it, block(me)]
        return remote(part, part, vec_send.at[it, k], vec_recv.at[it, k], {"sec": target(k)})

    def vec_pass(it, k):
        part = whole.at[it, block(source(k))]
        return remote(part, part, fwd_send.at[it, k], fwd_recv.at[it, k], {"sec": partner})

    def part_copy(slot, k):
        part = parts.at[slot, me]
        return remote(part, part, part_send.at[slot, k], part_recv.at[slot, k], {"sec": lax.rem(me + k, n)})

    def fold(value):
        total = value[0:8]
        for r in range(8, rows, 8):
            total = total + value[r : r + 8]
        short = total[:, 0:128]
        for c in range(128, value.shape[1], 128):
            short = short + total[:, c : c + 128]
        return short

    def send_part(slot, tile):
        parts[slot, me] = tile
        for k in range(1, n):
            part_copy(slot, k).start()

    def total_of(slot):
        for k in range(1, n):
            part_copy(slot, k).wait()
        total = parts[slot, 0]
        for j in range(1, n):
            total = total + parts[slot, j]
        return jnp.sum(total)

    def send_vector(it):
        for t in range(0, width, TILE):
            whole[it, block(me), t : t + TILE] = vector[:, t : t + TILE].astype(jnp.bfloat16)
        for k in range(1, chips):
            vec_copy(it, k).start()
        vec_pass(it, 0).start()

    for copy in shifts:
        copy.start()

    tile = jnp.zeros((8, 128), jnp.float32)
    for t in range(0, width, TILE):
        piece = start_ref[:, t : t + TILE]
        vector[:, t : t + TILE] = piece
        previous[:, t : t + TILE] = jnp.zeros_like(piece)
        tile = tile + fold(piece * piece)
    send_part(0, tile)
    send_vector(0)

    for c in range(3):
        shifts[c].wait()
        for k in range(1, chips):
            right_copy(c, k, me).start()
        right_pass(c, 0).start()
        if c == 2:
            left_copy.start()
        if c > 0:
            for k in range(1, chips):
                right_copy(c - 1, k, me).wait()
                right_pass(c - 1, k).start()
    for k in range(1, chips):
        right_copy(2, k, me).wait()
        right_pass(2, k).start()
    for c in range(3):
        for k in range(chips):
            right_pass(c, k).wait()

    charges = row_ref[...]

    @pl.loop(0, width // 128)
    def _(b):
        lines = pl.ds(pl.multiple_of(b * 128, 128), 128)
        step = charges - col_ref[lines, :]
        value = raw[0, lines, :].astype(jnp.float32)
        split[0, lines, :] = jnp.where(step == 0, value, 0.0).astype(jnp.bfloat16)
        split[1, lines, :] = jnp.where(step == 1, value, 0.0).astype(jnp.bfloat16)
        split[2, lines, :] = jnp.where(step == -1, value, 0.0).astype(jnp.bfloat16)

    left_copy.wait()

    def iteration(it, carry):
        def at(t):
            return pl.ds(pl.multiple_of(t * TILE, TILE), TILE)

        for k in range(chips):
            if k > 0:
                vec_copy(it, k).wait()
                vec_pass(it, k).start()
            vec_pass(it, k).wait()
            chip = lax.rem(me // 2 - k + chips, chips)
            span = pl.ds(pl.multiple_of(chip * 2 * rows, 2 * rows), 2 * rows)

            @pl.loop(0, width // TILE)
            def _(t, k=k, span=span):
                product = jnp.dot(
                    left_buf[:, span], whole[it, span, at(t)], preferred_element_type=jnp.float32
                )
                if k > 0:
                    product = product + first[:, at(t)]
                first[:, at(t)] = product

        size = jnp.sqrt(jnp.full((1, 128), total_of(2 * it) + EPS, jnp.float32))
        beta_ref[pl.ds(it, 1), :] = size
        size = size[:, 0:1]
        inverse = 1.0 / size

        @pl.loop(0, width // TILE)
        def _(t):
            gap = row_ref[:, at(t)] - mine_ref[...]
            up, down = gap == 1, gap == 0
            allowed = jnp.logical_or(up, down)
            spin = jnp.where(up, 0.5, -0.5)
            a = first[0:rows, at(t)] * inverse
            b = first[rows : 2 * rows, at(t)] * inverse
            c = first[2 * rows : 3 * rows, at(t)] * inverse
            half = 0.5 * c
            mixed[0, :, at(t)] = jnp.where(allowed, a + spin * b, 0.0).astype(jnp.bfloat16)
            mixed[1, :, at(t)] = jnp.where(up, half, 0.0).astype(jnp.bfloat16)
            mixed[2, :, at(t)] = jnp.where(down, half, 0.0).astype(jnp.bfloat16)
            mixed[3, :, at(t)] = jnp.where(allowed, spin * c, 0.0).astype(jnp.bfloat16)
            mixed[4, :, at(t)] = jnp.where(allowed, c, 0.0).astype(jnp.bfloat16)
            current[:, at(t)] = vector[:, at(t)] * inverse

        def second(t, tile):
            image = jnp.dot(mixed[0], split[0, :, at(t)], preferred_element_type=jnp.float32)
            image = image + jnp.dot(mixed[1], split[1, :, at(t)], preferred_element_type=jnp.float32)
            image = image + jnp.dot(mixed[2], split[2, :, at(t)], preferred_element_type=jnp.float32)
            image = image + jnp.dot(mixed[3], raw[1, :, at(t)], preferred_element_type=jnp.float32)
            image = image + jnp.dot(mixed[4], raw[2, :, at(t)], preferred_element_type=jnp.float32)
            gap = row_ref[:, at(t)] - mine_ref[...]
            allowed = jnp.logical_or(gap == 1, gap == 0)
            residual = jnp.where(allowed, image, 0.0) - size * previous[:, at(t)]
            vector[:, at(t)] = residual
            return tile + fold(residual * current[:, at(t)])

        tile = lax.fori_loop(0, width // TILE, second, jnp.zeros((8, 128), jnp.float32))
        send_part(2 * it + 1, tile)
        alpha = jnp.full((1, 1), total_of(2 * it + 1), jnp.float32)

        def finish(t, tile):
            now = current[:, at(t)]
            residual = vector[:, at(t)] - alpha * now
            vector[:, at(t)] = residual
            previous[:, at(t)] = now
            return tile + fold(residual * residual)

        tile = lax.fori_loop(0, width // TILE, finish, jnp.zeros((8, 128), jnp.float32))
        send_part(2 * it + 2, tile)

        @pl.when(it < ITERS - 1)
        def _():
            send_vector(it + 1)

        return carry

    lax.fori_loop(0, ITERS, iteration, 0)

    size = jnp.sqrt(jnp.full((1, 128), total_of(2 * ITERS) + EPS, jnp.float32))
    beta_ref[ITERS : ITERS + 1, :] = size
    scale = CHI / size[:, 0:1]
    for t in range(0, width, TILE):
        final_ref[:, t : t + TILE] = vector[:, t : t + TILE] * scale


def on_device(n, segs, start_vector, left_env, right_env, charge_left, charge_right):
    rows, width = left_env.shape[2], left_env.shape[3]
    left = merged(left_env[0]).reshape(3 * rows, width)
    right = merged(right_env[0])
    line = charge_right[0][None, :]
    mine = charge_left[0][:, None]
    gap = line - mine
    down, up = gap == 0, gap == 1
    start = jnp.where(down, start_vector[0, :, 0], jnp.where(up, start_vector[0, :, 1], 0.0))
    slots = 2 * ITERS + 1
    chips = n // 2
    dma = pltpu.SemaphoreType.DMA
    final, betas = pl.pallas_call(
        functools.partial(kernel, n, segs),
        out_shape=(
            jax.ShapeDtypeStruct((rows, width), jnp.float32),
            jax.ShapeDtypeStruct((8, 128), jnp.float32),
        ),
        in_specs=[pl.BlockSpec(memory_space=pltpu.VMEM)] * 6,
        out_specs=[pl.BlockSpec(memory_space=pltpu.VMEM)] * 2,
        scratch_shapes=[
            pltpu.VMEM((3 * rows, width), jnp.bfloat16),
            pltpu.VMEM((3, n * rows, width), jnp.bfloat16),
            pltpu.VMEM((3, n * rows, width), jnp.bfloat16),
            pltpu.VMEM((ITERS, n * rows, width), jnp.bfloat16),
            pltpu.VMEM((3 * rows, width), jnp.float32),
            pltpu.VMEM((5, rows, width), jnp.bfloat16),
            pltpu.VMEM((rows, width), jnp.float32),
            pltpu.VMEM((rows, width), jnp.float32),
            pltpu.VMEM((rows, width), jnp.float32),
            pltpu.VMEM((slots, n, 8, 128), jnp.float32),
            dma,
            dma,
            dma((3,)),
            dma((3,)),
            dma((3, chips)),
            dma((3, chips)),
            dma((3, chips)),
            dma((3, chips)),
            dma((ITERS, chips)),
            dma((ITERS, chips)),
            dma((ITERS, chips)),
            dma((ITERS, chips)),
            dma((slots, n)),
            dma((slots, n)),
        ],
        compiler_params=pltpu.CompilerParams(
            collective_id=0, has_side_effects=True, vmem_limit_bytes=48 * 1024 * 1024
        ),
    )(left, right, start, line, line.reshape(width, 1), mine)
    full = jnp.stack([jnp.where(down, final, 0.0), jnp.where(up, final, 0.0)], axis=1)
    return full[None], betas[None, 1 : ITERS + 1, 0]


def solution(mesh):
    return jax.shard_map(
        functools.partial(on_device, mesh.shape["sec"], mesh.shape["seg"]),
        mesh=mesh,
        in_specs=(
            P("seg", "sec", None, None),
            P("seg", None, "sec", None),
            P("seg", None, "sec", None),
            P("seg", "sec"),
            P("seg", None),
        ),
        out_specs=(P("seg", "sec", None, None), P("seg", None)),
        check_vma=False,
    )
```

```python
import functools

import jax
import jax.numpy as jnp
from jax import lax
from jax.experimental import pallas as pl
from jax.experimental.pallas import tpu as pltpu
from jax.sharding import PartitionSpec as P

CHI = 1024
ITERS = 4
EPS = 1e-06
MESH = pl.DeviceIdType.MESH
TILE = 256


def merged(env):
    return jnp.stack([env[0] + env[1] + env[2], env[3], env[4]])


def kernel(
    n,
    segs,
    left_ref,
    right_ref,
    start_ref,
    row_ref,
    col_ref,
    mine_ref,
    final_ref,
    beta_ref,
    left_buf,
    raw,
    split,
    whole,
    first,
    mixed,
    current,
    previous,
    vector,
    parts,
    left_send,
    left_recv,
    shift_send,
    shift_recv,
    right_send,
    right_recv,
    pass_send,
    pass_recv,
    vec_send,
    vec_recv,
    fwd_send,
    fwd_recv,
    part_send,
    part_recv,
):
    me = lax.axis_index("sec")
    seg = lax.axis_index("seg")
    rows, width = start_ref.shape
    chips = n // 2
    partner = me + 1 - 2 * lax.rem(me, 2)
    after, before = lax.rem(seg + 1, segs), lax.rem(seg + segs - 1, segs)

    square = chips == 4
    pieces = 7 if square else chips
    if square:
        column = lax.rem(me // 2, 2)
        line = me // 4
        beside = me + 2 - 4 * column
        above = me + 4 - 8 * line
        across = above + 2 - 4 * column

    def source(k):
        return lax.rem(me - 2 * k + n, n)

    def target(k):
        return lax.rem(me + 2 * k, n)

    def block(index):
        return pl.ds(pl.multiple_of(index * rows, rows), rows)

    barrier = pltpu.get_barrier_semaphore()
    for k in range(1, n):
        pl.semaphore_signal(barrier, inc=1, device_id={"sec": lax.rem(me + k, n)}, device_id_type=MESH)
    for other in (after, before):
        pl.semaphore_signal(barrier, inc=1, device_id={"seg": other}, device_id_type=MESH)
    pl.semaphore_wait(barrier, n + 1)

    def remote(src, dst, send, recv, where):
        return pltpu.make_async_remote_copy(
            src_ref=src, dst_ref=dst, send_sem=send, recv_sem=recv, device_id=where, device_id_type=MESH
        )

    left_copy = remote(left_ref, left_buf, left_send, left_recv, {"seg": after})
    shifts = [
        remote(right_ref.at[c], raw.at[c, block(me)], shift_send.at[c], shift_recv.at[c], {"seg": before})
        for c in range(3)
    ]

    class Gather:
        def __init__(self, buf, i, send, recv, fsend, frecv):
            self.buf, self.i = buf, i
            self.sems = send, recv, fsend, frecv

        def move(self, j, owner, half, where, forward=False):
            send, recv = self.sems[2:] if forward else self.sems[:2]
            if half is None:
                part = self.buf.at[self.i, block(owner)]
            else:
                size = rows // 2
                part = self.buf.at[self.i, pl.ds(pl.multiple_of(owner * rows + half * size, size), size)]
            return remote(part, part, send.at[self.i, j], recv.at[self.i, j], {"sec": where})

        def direct(self, j):
            if not square:
                return self.move(j, me, None, target(j))
            return self.move(j, me, (0, 1, 1, 0)[j - 1], (beside, above)[(j - 1) % 2])

        def relay(self, j):
            return self.move(5 + j, (beside, above)[j], j, (above, beside)[j])

        def passed(self, j):
            if not square:
                return self.move(j, source(j), None, partner, True)
            owner = (me, beside, above, beside, above, across, across)[j]
            return self.move(j, owner, (None, 0, 1, 1, 0, 0, 1)[j], partner, True)

        def begin(self):
            for j in range(1, 5 if square else chips):
                self.direct(j).start()
            self.passed(0).start()

        def spread(self):
            for j in range(1, 5 if square else chips):
                self.direct(j).wait()
                if square and j < 3:
                    self.relay(j - 1).start()
                self.passed(j).start()

        def last(self):
            if square:
                for j in range(2):
                    self.relay(j).wait()
                    self.passed(5 + j).start()

    def right_gather(c):
        return Gather(raw, c, right_send, right_recv, pass_send, pass_recv)

    def vector_gather(it):
        return Gather(whole, it, vec_send, vec_recv, fwd_send, fwd_recv)

    def part_copy(slot, k):
        part = parts.at[slot, me]
        return remote(part, part, part_send.at[slot, k], part_recv.at[slot, k], {"sec": lax.rem(me + k, n)})

    def fold(value):
        total = value[0:8]
        for r in range(8, rows, 8):
            total = total + value[r : r + 8]
        short = total[:, 0:128]
        for c in range(128, value.shape[1], 128):
            short = short + total[:, c : c + 128]
        return short

    def send_part(slot, tile, other=None):
        parts[slot, me, 0:8] = tile
        parts[slot, me, 8:16] = jnp.zeros_like(tile) if other is None else other
        for k in range(1, n):
            part_copy(slot, k).start()

    def totals_of(slot):
        for k in range(1, n):
            part_copy(slot, k).wait()
        total = parts[slot, 0]
        for j in range(1, n):
            total = total + parts[slot, j]
        return jnp.sum(total[0:8]), jnp.sum(total[8:16])

    def send_vector(it, factor):
        for t in range(0, width, TILE):
            whole[it, block(me), t : t + TILE] = (vector[:, t : t + TILE] * factor).astype(jnp.bfloat16)
        vector_gather(it).begin()

    def root(value):
        return jnp.sqrt(jnp.full((1, 128), value + EPS, jnp.float32))

    for copy in shifts:
        copy.start()

    tile = jnp.zeros((8, 128), jnp.float32)
    for t in range(0, width, TILE):
        piece = start_ref[:, t : t + TILE]
        vector[:, t : t + TILE] = piece
        previous[:, t : t + TILE] = jnp.zeros_like(piece)
        tile = tile + fold(piece * piece)
    send_part(2 * ITERS + 1, tile)
    guess = root(totals_of(2 * ITERS + 1)[0])
    send_part(0, tile)
    send_vector(0, 1.0 / guess[:, 0:1])

    for c in range(3):
        shifts[c].wait()
        right_gather(c).begin()
        if c == 2:
            left_copy.start()
        if c > 0:
            right_gather(c - 1).spread()
        if c > 1:
            right_gather(c - 2).last()
    right_gather(2).spread()
    right_gather(1).last()
    right_gather(2).last()
    for c in range(3):
        for j in range(pieces):
            right_gather(c).passed(j).wait()

    charges = row_ref[...]

    @pl.loop(0, width // 128)
    def _(b):
        lines = pl.ds(pl.multiple_of(b * 128, 128), 128)
        step = charges - col_ref[lines, :]
        value = raw[0, lines, :].astype(jnp.float32)
        split[0, lines, :] = jnp.where(step == 0, value, 0.0).astype(jnp.bfloat16)
        split[1, lines, :] = jnp.where(step == 1, value, 0.0).astype(jnp.bfloat16)
        split[2, lines, :] = jnp.where(step == -1, value, 0.0).astype(jnp.bfloat16)

    left_copy.wait()

    def iteration(it, guess):
        def at(t):
            return pl.ds(pl.multiple_of(t * TILE, TILE), TILE)

        def contract(owner, fresh):
            span = pl.ds(pl.multiple_of(owner // 2 * (2 * rows), 2 * rows), 2 * rows)

            @pl.loop(0, width // TILE)
            def _(t):
                product = jnp.dot(
                    left_buf[:, span], whole[it, span, at(t)], preferred_element_type=jnp.float32
                )
                if not fresh:
                    product = product + first[:, at(t)]
                first[:, at(t)] = product

        gather = vector_gather(it)
        gather.passed(0).wait()
        contract(me, True)
        gather.spread()
        if square:
            for owner, own in ((beside, (1, 3)), (above, (2, 4))):
                for j in own:
                    gather.passed(j).wait()
                contract(owner, False)
            gather.last()
            for j in (5, 6):
                gather.passed(j).wait()
            contract(across, False)
        else:
            for k in range(1, chips):
                gather.passed(k).wait()
                contract(source(k), False)

        size = root(totals_of(2 * it)[0])
        beta_ref[pl.ds(it, 1), :] = size
        size = size[:, 0:1]
        inverse = 1.0 / size
        ratio = guess[:, 0:1] * inverse

        @pl.loop(0, width // TILE)
        def _(t):
            gap = row_ref[:, at(t)] - mine_ref[...]
            up, down = gap == 1, gap == 0
            allowed = jnp.logical_or(up, down)
            spin = jnp.where(up, 0.5, -0.5)
            a = first[0:rows, at(t)] * ratio
            b = first[rows : 2 * rows, at(t)] * ratio
            c = first[2 * rows : 3 * rows, at(t)] * ratio
            half = 0.5 * c
            mixed[0, :, at(t)] = jnp.where(allowed, a + spin * b, 0.0).astype(jnp.bfloat16)
            mixed[1, :, at(t)] = jnp.where(up, half, 0.0).astype(jnp.bfloat16)
            mixed[2, :, at(t)] = jnp.where(down, half, 0.0).astype(jnp.bfloat16)
            mixed[3, :, at(t)] = jnp.where(allowed, spin * c, 0.0).astype(jnp.bfloat16)
            mixed[4, :, at(t)] = jnp.where(allowed, c, 0.0).astype(jnp.bfloat16)
            current[:, at(t)] = vector[:, at(t)] * inverse

        def second(t, tiles):
            image = jnp.dot(mixed[0], split[0, :, at(t)], preferred_element_type=jnp.float32)
            image = image + jnp.dot(mixed[1], split[1, :, at(t)], preferred_element_type=jnp.float32)
            image = image + jnp.dot(mixed[2], split[2, :, at(t)], preferred_element_type=jnp.float32)
            image = image + jnp.dot(mixed[3], raw[1, :, at(t)], preferred_element_type=jnp.float32)
            image = image + jnp.dot(mixed[4], raw[2, :, at(t)], preferred_element_type=jnp.float32)
            gap = row_ref[:, at(t)] - mine_ref[...]
            allowed = jnp.logical_or(gap == 1, gap == 0)
            residual = jnp.where(allowed, image, 0.0) - size * previous[:, at(t)]
            vector[:, at(t)] = residual
            return tiles[0] + fold(residual * current[:, at(t)]), tiles[1] + fold(residual * residual)

        zero = jnp.zeros((8, 128), jnp.float32)
        send_part(2 * it + 1, *lax.fori_loop(0, width // TILE, second, (zero, zero)))
        product, square_sum = totals_of(2 * it + 1)
        alpha = jnp.full((1, 1), product, jnp.float32)
        guess = root(jnp.maximum(square_sum - product * product, 0.0))

        def finish(t, tile):
            now = current[:, at(t)]
            residual = vector[:, at(t)] - alpha * now
            vector[:, at(t)] = residual
            previous[:, at(t)] = now
            return tile + fold(residual * residual)

        tile = lax.fori_loop(0, width // TILE, finish, zero)

        @pl.when(it < ITERS - 1)
        def _():
            send_vector(it + 1, 1.0 / guess[:, 0:1])

        send_part(2 * it + 2, tile)
        return guess

    lax.fori_loop(0, ITERS, iteration, guess)

    size = root(totals_of(2 * ITERS)[0])
    beta_ref[ITERS : ITERS + 1, :] = size
    scale = CHI / size[:, 0:1]
    for t in range(0, width, TILE):
        final_ref[:, t : t + TILE] = vector[:, t : t + TILE] * scale


def on_device(n, segs, start_vector, left_env, right_env, charge_left, charge_right):
    rows, width = left_env.shape[2], left_env.shape[3]
    left = merged(left_env[0]).reshape(3 * rows, width)
    right = merged(right_env[0])
    line = charge_right[0][None, :]
    mine = charge_left[0][:, None]
    gap = line - mine
    down, up = gap == 0, gap == 1
    start = jnp.where(down, start_vector[0, :, 0], jnp.where(up, start_vector[0, :, 1], 0.0))
    slots = 2 * ITERS + 2
    pieces = 7 if n == 8 else n // 2
    dma = pltpu.SemaphoreType.DMA
    final, betas = pl.pallas_call(
        functools.partial(kernel, n, segs),
        out_shape=(
            jax.ShapeDtypeStruct((rows, width), jnp.float32),
            jax.ShapeDtypeStruct((8, 128), jnp.float32),
        ),
        in_specs=[pl.BlockSpec(memory_space=pltpu.VMEM)] * 6,
        out_specs=[pl.BlockSpec(memory_space=pltpu.VMEM)] * 2,
        scratch_shapes=[
            pltpu.VMEM((3 * rows, width), jnp.bfloat16),
            pltpu.VMEM((3, n * rows, width), jnp.bfloat16),
            pltpu.VMEM((3, n * rows, width), jnp.bfloat16),
            pltpu.VMEM((ITERS, n * rows, width), jnp.bfloat16),
            pltpu.VMEM((3 * rows, width), jnp.float32),
            pltpu.VMEM((5, rows, width), jnp.bfloat16),
            pltpu.VMEM((rows, width), jnp.float32),
            pltpu.VMEM((rows, width), jnp.float32),
            pltpu.VMEM((rows, width), jnp.float32),
            pltpu.VMEM((slots, n, 16, 128), jnp.float32),
            dma,
            dma,
            dma((3,)),
            dma((3,)),
            dma((3, pieces)),
            dma((3, pieces)),
            dma((3, pieces)),
            dma((3, pieces)),
            dma((ITERS, pieces)),
            dma((ITERS, pieces)),
            dma((ITERS, pieces)),
            dma((ITERS, pieces)),
            dma((slots, n)),
            dma((slots, n)),
        ],
        compiler_params=pltpu.CompilerParams(
            collective_id=0, has_side_effects=True, vmem_limit_bytes=48 * 1024 * 1024
        ),
    )(left, right, start, line, line.reshape(width, 1), mine)
    full = jnp.stack([jnp.where(down, final, 0.0), jnp.where(up, final, 0.0)], axis=1)
    return full[None], betas[None, 1 : ITERS + 1, 0]


def solution(mesh):
    return jax.shard_map(
        functools.partial(on_device, mesh.shape["sec"], mesh.shape["seg"]),
        mesh=mesh,
        in_specs=(
            P("seg", "sec", None, None),
            P("seg", None, "sec", None),
            P("seg", None, "sec", None),
            P("seg", "sec"),
            P("seg", None),
        ),
        out_specs=(P("seg", "sec", None, None), P("seg", None)),
        check_vma=False,
    )
```

```python
import functools

import jax
import jax.numpy as jnp
from jax import lax
from jax.experimental import pallas as pl
from jax.experimental.pallas import tpu as pltpu
from jax.sharding import PartitionSpec as P

CHI = 1024
ITERS = 4
EPS = 1e-06
MESH = pl.DeviceIdType.MESH
TILE = 1024


def merged(env):
    return jnp.stack([env[0] + env[1] + env[2], env[3], env[4]])


def kernel(
    n,
    segs,
    left_ref,
    right_ref,
    start_ref,
    row_ref,
    col_ref,
    mine_ref,
    final_ref,
    beta_ref,
    left_buf,
    raw,
    split,
    whole,
    first,
    mixed,
    current,
    previous,
    vector,
    parts,
    left_send,
    left_recv,
    shift_send,
    shift_recv,
    right_send,
    right_recv,
    pass_send,
    pass_recv,
    vec_send,
    vec_recv,
    fwd_send,
    fwd_recv,
    part_send,
    part_recv,
):
    me = lax.axis_index("sec")
    seg = lax.axis_index("seg")
    rows, width = start_ref.shape
    chips = n // 2
    partner = me + 1 - 2 * lax.rem(me, 2)
    after, before = lax.rem(seg + 1, segs), lax.rem(seg + segs - 1, segs)

    square = chips == 4
    pieces = 7 if square else chips
    if square:
        column = lax.rem(me // 2, 2)
        line = me // 4
        beside = me + 2 - 4 * column
        above = me + 4 - 8 * line
        across = above + 2 - 4 * column

    def source(k):
        return lax.rem(me - 2 * k + n, n)

    def target(k):
        return lax.rem(me + 2 * k, n)

    def block(index):
        return pl.ds(pl.multiple_of(index * rows, rows), rows)

    barrier = pltpu.get_barrier_semaphore()
    for k in range(1, n):
        pl.semaphore_signal(barrier, inc=1, device_id={"sec": lax.rem(me + k, n)}, device_id_type=MESH)
    for other in (after, before):
        pl.semaphore_signal(barrier, inc=1, device_id={"seg": other}, device_id_type=MESH)
    pl.semaphore_wait(barrier, n + 1)

    def remote(src, dst, send, recv, where):
        return pltpu.make_async_remote_copy(
            src_ref=src, dst_ref=dst, send_sem=send, recv_sem=recv, device_id=where, device_id_type=MESH
        )

    left_copy = remote(left_ref, left_buf, left_send, left_recv, {"seg": after})
    shifts = [
        remote(right_ref.at[c], raw.at[c, block(me)], shift_send.at[c], shift_recv.at[c], {"seg": before})
        for c in range(3)
    ]

    class Gather:
        def __init__(self, buf, i, send, recv, fsend, frecv):
            self.buf, self.i = buf, i
            self.sems = send, recv, fsend, frecv

        def move(self, j, owner, half, where, forward=False):
            send, recv = self.sems[2:] if forward else self.sems[:2]
            if half is None:
                part = self.buf.at[self.i, block(owner)]
            else:
                size = rows // 2
                part = self.buf.at[self.i, pl.ds(pl.multiple_of(owner * rows + half * size, size), size)]
            return remote(part, part, send.at[self.i, j], recv.at[self.i, j], {"sec": where})

        def direct(self, j):
            if not square:
                return self.move(j, me, None, target(j))
            return self.move(j, me, (0, 1, 1, 0)[j - 1], (beside, above)[(j - 1) % 2])

        def relay(self, j):
            return self.move(5 + j, (beside, above)[j], j, (above, beside)[j])

        def passed(self, j):
            if not square:
                return self.move(j, source(j), None, partner, True)
            owner = (me, beside, above, beside, above, across, across)[j]
            return self.move(j, owner, (None, 0, 1, 1, 0, 0, 1)[j], partner, True)

        def begin(self):
            for j in range(1, 5 if square else chips):
                self.direct(j).start()
            self.passed(0).start()

        def spread(self):
            for j in range(1, 5 if square else chips):
                self.direct(j).wait()
                if square and j < 3:
                    self.relay(j - 1).start()
                self.passed(j).start()

        def last(self):
            if square:
                for j in range(2):
                    self.relay(j).wait()
                    self.passed(5 + j).start()

    def right_gather(c):
        return Gather(raw, c, right_send, right_recv, pass_send, pass_recv)

    def vector_gather(it):
        return Gather(whole, it, vec_send, vec_recv, fwd_send, fwd_recv)

    def part_copy(slot, k):
        part = parts.at[slot, me]
        return remote(part, part, part_send.at[slot, k], part_recv.at[slot, k], {"sec": lax.rem(me + k, n)})

    def fold(value):
        total = value[0:8]
        for r in range(8, rows, 8):
            total = total + value[r : r + 8]
        short = total[:, 0:128]
        for c in range(128, value.shape[1], 128):
            short = short + total[:, c : c + 128]
        return short

    def send_part(slot, tile, other=None):
        parts[slot, me, 0:8] = tile
        parts[slot, me, 8:16] = jnp.zeros_like(tile) if other is None else other
        for k in range(1, n):
            part_copy(slot, k).start()

    def totals_of(slot):
        for k in range(1, n):
            part_copy(slot, k).wait()
        total = parts[slot, 0]
        for j in range(1, n):
            total = total + parts[slot, j]
        return jnp.sum(total[0:8]), jnp.sum(total[8:16])

    def send_vector(it, factor):
        for t in range(0, width, TILE):
            whole[it, block(me), t : t + TILE] = (vector[:, t : t + TILE] * factor).astype(jnp.bfloat16)
        vector_gather(it).begin()

    def root(value):
        return jnp.sqrt(jnp.full((1, 128), value + EPS, jnp.float32))

    for copy in shifts:
        copy.start()

    tile = jnp.zeros((8, 128), jnp.float32)
    for t in range(0, width, TILE):
        piece = start_ref[:, t : t + TILE]
        vector[:, t : t + TILE] = piece
        previous[:, t : t + TILE] = jnp.zeros_like(piece)
        tile = tile + fold(piece * piece)
    send_part(2 * ITERS + 1, tile)
    guess = root(totals_of(2 * ITERS + 1)[0])
    send_part(0, tile)
    send_vector(0, 1.0 / guess[:, 0:1])

    for c in range(3):
        shifts[c].wait()
        right_gather(c).begin()
        if c == 1:
            left_copy.start()
        if c > 0:
            right_gather(c - 1).spread()
        if c > 1:
            right_gather(c - 2).last()
    right_gather(2).spread()
    right_gather(1).last()
    right_gather(2).last()
    for c in range(3):
        for j in range(pieces):
            right_gather(c).passed(j).wait()

    charges = row_ref[...]

    @pl.loop(0, width // 128)
    def _(b):
        lines = pl.ds(pl.multiple_of(b * 128, 128), 128)
        step = charges - col_ref[lines, :]
        value = raw[0, lines, :].astype(jnp.float32)
        split[0, lines, :] = jnp.where(step == 0, value, 0.0).astype(jnp.bfloat16)
        split[1, lines, :] = jnp.where(step == 1, value, 0.0).astype(jnp.bfloat16)
        split[2, lines, :] = jnp.where(step == -1, value, 0.0).astype(jnp.bfloat16)

    left_copy.wait()

    def iteration(it, guess):
        def at(t):
            return pl.ds(pl.multiple_of(t * TILE, TILE), TILE)

        def contract(owner, fresh):
            span = pl.ds(pl.multiple_of(owner // 2 * (2 * rows), 2 * rows), 2 * rows)

            @pl.loop(0, width // TILE)
            def _(t):
                product = jnp.dot(
                    left_buf[:, span], whole[it, span, at(t)], preferred_element_type=jnp.float32
                )
                if not fresh:
                    product = product + first[:, at(t)]
                first[:, at(t)] = product

        gather = vector_gather(it)
        gather.passed(0).wait()
        contract(me, True)
        gather.spread()
        if square:
            for owner, own in ((beside, (1, 3)), (above, (2, 4))):
                for j in own:
                    gather.passed(j).wait()
                contract(owner, False)
            gather.last()
            for j in (5, 6):
                gather.passed(j).wait()
            contract(across, False)
        else:
            for k in range(1, chips):
                gather.passed(k).wait()
                contract(source(k), False)

        size = root(totals_of(2 * it)[0])
        beta_ref[pl.ds(it, 1), :] = size
        size = size[:, 0:1]
        inverse = 1.0 / size
        ratio = guess[:, 0:1] * inverse

        @pl.loop(0, width // TILE)
        def _(t):
            gap = row_ref[:, at(t)] - mine_ref[...]
            up, down = gap == 1, gap == 0
            allowed = jnp.logical_or(up, down)
            spin = jnp.where(up, 0.5, -0.5)
            a = first[0:rows, at(t)] * ratio
            b = first[rows : 2 * rows, at(t)] * ratio
            c = first[2 * rows : 3 * rows, at(t)] * ratio
            half = 0.5 * c
            mixed[0, :, at(t)] = jnp.where(allowed, a + spin * b, 0.0).astype(jnp.bfloat16)
            mixed[1, :, at(t)] = jnp.where(up, half, 0.0).astype(jnp.bfloat16)
            mixed[2, :, at(t)] = jnp.where(down, half, 0.0).astype(jnp.bfloat16)
            mixed[3, :, at(t)] = jnp.where(allowed, spin * c, 0.0).astype(jnp.bfloat16)
            mixed[4, :, at(t)] = jnp.where(allowed, c, 0.0).astype(jnp.bfloat16)
            current[:, at(t)] = vector[:, at(t)] * inverse

        def second(t, tiles):
            image = jnp.dot(mixed[0], split[0, :, at(t)], preferred_element_type=jnp.float32)
            image = image + jnp.dot(mixed[1], split[1, :, at(t)], preferred_element_type=jnp.float32)
            image = image + jnp.dot(mixed[2], split[2, :, at(t)], preferred_element_type=jnp.float32)
            image = image + jnp.dot(mixed[3], raw[1, :, at(t)], preferred_element_type=jnp.float32)
            image = image + jnp.dot(mixed[4], raw[2, :, at(t)], preferred_element_type=jnp.float32)
            gap = row_ref[:, at(t)] - mine_ref[...]
            allowed = jnp.logical_or(gap == 1, gap == 0)
            residual = jnp.where(allowed, image, 0.0) - size * previous[:, at(t)]
            vector[:, at(t)] = residual
            return tiles[0] + fold(residual * current[:, at(t)]), tiles[1] + fold(residual * residual)

        zero = jnp.zeros((8, 128), jnp.float32)
        send_part(2 * it + 1, *lax.fori_loop(0, width // TILE, second, (zero, zero)))
        product, square_sum = totals_of(2 * it + 1)
        alpha = jnp.full((1, 1), product, jnp.float32)
        guess = root(jnp.maximum(square_sum - product * product, 0.0))

        def finish(t, tile):
            now = current[:, at(t)]
            residual = vector[:, at(t)] - alpha * now
            vector[:, at(t)] = residual
            previous[:, at(t)] = now
            return tile + fold(residual * residual)

        tile = lax.fori_loop(0, width // TILE, finish, zero)

        @pl.when(it < ITERS - 1)
        def _():
            send_vector(it + 1, 1.0 / guess[:, 0:1])

        send_part(2 * it + 2, tile)
        return guess

    lax.fori_loop(0, ITERS, iteration, guess)

    size = root(totals_of(2 * ITERS)[0])
    beta_ref[ITERS : ITERS + 1, :] = size
    scale = CHI / size[:, 0:1]
    for t in range(0, width, TILE):
        final_ref[:, t : t + TILE] = vector[:, t : t + TILE] * scale


def on_device(n, segs, start_vector, left_env, right_env, charge_left, charge_right):
    rows, width = left_env.shape[2], left_env.shape[3]
    left = merged(left_env[0]).reshape(3 * rows, width)
    right = merged(right_env[0])
    line = charge_right[0][None, :]
    mine = charge_left[0][:, None]
    gap = line - mine
    down, up = gap == 0, gap == 1
    start = jnp.where(down, start_vector[0, :, 0], jnp.where(up, start_vector[0, :, 1], 0.0))
    slots = 2 * ITERS + 2
    pieces = 7 if n == 8 else n // 2
    dma = pltpu.SemaphoreType.DMA
    final, betas = pl.pallas_call(
        functools.partial(kernel, n, segs),
        out_shape=(
            jax.ShapeDtypeStruct((rows, width), jnp.float32),
            jax.ShapeDtypeStruct((8, 128), jnp.float32),
        ),
        in_specs=[pl.BlockSpec(memory_space=pltpu.VMEM)] * 6,
        out_specs=[pl.BlockSpec(memory_space=pltpu.VMEM)] * 2,
        scratch_shapes=[
            pltpu.VMEM((3 * rows, width), jnp.bfloat16),
            pltpu.VMEM((3, n * rows, width), jnp.bfloat16),
            pltpu.VMEM((3, n * rows, width), jnp.bfloat16),
            pltpu.VMEM((ITERS, n * rows, width), jnp.bfloat16),
            pltpu.VMEM((3 * rows, width), jnp.float32),
            pltpu.VMEM((5, rows, width), jnp.bfloat16),
            pltpu.VMEM((rows, width), jnp.float32),
            pltpu.VMEM((rows, width), jnp.float32),
            pltpu.VMEM((rows, width), jnp.float32),
            pltpu.VMEM((slots, n, 16, 128), jnp.float32),
            dma,
            dma,
            dma((3,)),
            dma((3,)),
            dma((3, pieces)),
            dma((3, pieces)),
            dma((3, pieces)),
            dma((3, pieces)),
            dma((ITERS, pieces)),
            dma((ITERS, pieces)),
            dma((ITERS, pieces)),
            dma((ITERS, pieces)),
            dma((slots, n)),
            dma((slots, n)),
        ],
        compiler_params=pltpu.CompilerParams(
            collective_id=0, has_side_effects=True, vmem_limit_bytes=48 * 1024 * 1024
        ),
    )(left, right, start, line, line.reshape(width, 1), mine)
    full = jnp.stack([jnp.where(down, final, 0.0), jnp.where(up, final, 0.0)], axis=1)
    return full[None], betas[None, 1 : ITERS + 1, 0]


def solution(mesh):
    return jax.shard_map(
        functools.partial(on_device, mesh.shape["sec"], mesh.shape["seg"]),
        mesh=mesh,
        in_specs=(
            P("seg", "sec", None, None),
            P("seg", None, "sec", None),
            P("seg", None, "sec", None),
            P("seg", "sec"),
            P("seg", None),
        ),
        out_specs=(P("seg", "sec", None, None), P("seg", None)),
        check_vma=False,
    )
```
